32 devices in a mesh: groups: 2 (over x), seq: 16 (over z, y, core).
Axes of the slice: x: 2, y: 2, z: 4, core: 2. Of those that a mesh axis runs over, the one named last changes fastest.
Arguments:
- queries: bfloat16 [4096, 5120], P(('groups', 'seq')), parts along dimension 0, may hold values from -12 to 12
- keys: bfloat16 [4096, 5120], P(('groups', 'seq')), parts along dimension 0, may hold values from -12 to 12
- values: bfloat16 [4096, 5120], P(('groups', 'seq')), parts along dimension 0, may hold values from -6 to 6
- q_gain: float32 [5120], replicated, may hold values from 0.1 to 1.9
- k_gain: float32 [5120], replicated, may hold values from 0.1 to 1.9
- key_tiles: int32 [40, 16, 16], replicated, may hold values from 0 to 15, as said below
- key_count: int32 [40, 16], replicated, may hold values from 1 to 16
Outputs:
- attended: bfloat16 [4096, 5120], P(('groups', 'seq')), parts along dimension 0
The draws below stay inside these ranges and needn't reach their ends.
There are 2 independent parts, one for each index of `groups`. The reference program is written for one: setup_inputs(seed, part) draws one part's arguments, and reference() takes and returns one part's arrays. A program takes and returns all parts, laid end to end along the dimension named above; an argument that names none is the same for every part. Nothing has to cross between parts.
Inputs may be any that keep to these rules, and one draw needn't show every extreme that they name: key_tiles[h, t] holds 16 distinct tiles and its first entry is t itself.
All inputs are finite; a program needn't handle non-finite values.
Results may differ from the reference program's by a relative error of at most 0.012.
The reference program's roundings to bfloat16 on the way count: a program that leaves them out, or rounds other values in their place, can miss the bound.
Values may be sent and summed in bfloat16 or wider, within the bound.
A program may use at most 128 MiB of HBM per device.

```python
import math
import jax
import jax.numpy as jnp
from jax import lax

D = 5120
HEADS = 40
HEAD_DIM = 128
TILE = 128
KEEP = 16
TILES = 16
TOKENS = 2048


def pair_rows(key):
    key_parts = jax.random.split(jax.random.fold_in(key, 7), 3)
    col_scale = jnp.exp(jax.random.uniform(key_parts[0], (D,), jnp.float32, math.log(0.3), math.log(3.0)))
    query_rows = jnp.clip(jax.random.normal(key_parts[1], (TOKENS, D), jnp.float32), -4.0, 4.0) * col_scale
    key_rows = jnp.clip(jax.random.normal(key_parts[2], (TOKENS, D), jnp.float32), -4.0, 4.0) * col_scale
    return (query_rows, key_rows)


def draw_queries(key, part):
    return pair_rows(key)[0].astype(jnp.bfloat16)


def draw_keys(key, part):
    return pair_rows(key)[1].astype(jnp.bfloat16)


def draw_key_tiles(key, part):
    random_draws = jax.random.randint(jax.random.fold_in(key, 11), (HEADS, TILES, TILES), 0, 1 << 20)
    column = jnp.arange(TILES)
    ranking = random_draws * TILES + column[None, None, :]
    ranking = jnp.where(column[None, None, :] == column[None, :, None], 1 << 30, ranking)
    return lax.top_k(ranking, KEEP)[1].astype(jnp.int32)


def draw_key_count(key, part):
    key_parts = jax.random.split(jax.random.fold_in(key, 13), 3)
    lowest = jax.random.randint(key_parts[0], (HEADS, 1), 1, KEEP + 1)
    random_draws = jax.random.randint(key_parts[1], (HEADS, TILES), 0, 1 << 20)
    counts = random_draws % (KEEP - lowest + 1) + lowest
    places = jax.random.randint(key_parts[2], (2,), 0, HEADS * TILES)
    top_place = places[0]
    low_place = (places[0] + 1 + places[1] % (HEADS * TILES - 1)) % (HEADS * TILES)
    flattened = counts.reshape(-1)
    position = jnp.arange(HEADS * TILES)
    flattened = jnp.where(position == top_place, KEEP, jnp.where(position == low_place, 1, flattened))
    return flattened.reshape(HEADS, TILES).astype(jnp.int32)


def levels(stream_key, extent, shards, smallest, top_value):
    factor_of, own = 1.0, jax.random.fold_in(stream_key, 6)
    for axis_at, blocks in shards:
        draws = jnp.exp(jax.random.uniform(jax.random.fold_in(own, axis_at), (blocks,), jnp.float32, smallest / len(shards), top_value / len(shards)))
        factor_of = factor_of * jnp.repeat(draws, extent[axis_at] // blocks).reshape([-1 if axis == axis_at else 1 for axis in range(len(extent))])
    return factor_of


def gaussian(stream_key, dims, width, reach, cuts=(), kind=jnp.bfloat16):
    entries = jax.random.normal(stream_key, dims, jnp.float32) * width
    if len(cuts) > 0:
        entries = levels(stream_key, dims, cuts, -0.22, 0.18) * entries
    return jnp.clip(entries, min=-reach, max=reach).astype(kind)


def setup_inputs(seed: int = 0, part: int = 0) -> dict:
    arg_keys = jax.random.split(jax.random.key(seed), 8)
    part_splits = jax.random.split(jax.random.fold_in(arg_keys[7], part), 8)
    return {
        "queries": draw_queries(jax.random.fold_in(jax.random.fold_in(arg_keys[7], part), 71), part),
        "keys": draw_keys(jax.random.fold_in(jax.random.fold_in(arg_keys[7], part), 71), part),
        "values": gaussian(part_splits[2], (TOKENS, D), 1.0, 6.0, ((0, 16),)),
        "q_gain": jnp.clip(1.0 + 0.18 * jax.random.normal(arg_keys[3], (D,), jnp.float32), 0.1, 1.9),
        "k_gain": jnp.clip(1.0 + 0.18 * jax.random.normal(arg_keys[4], (D,), jnp.float32), 0.1, 1.9),
        "key_tiles": draw_key_tiles(jax.random.fold_in(arg_keys[7], 71), part),
        "key_count": draw_key_count(jax.random.fold_in(arg_keys[7], 71), part),
    }


def normed(rows, gain):
    values32 = rows.astype(jnp.float32)
    factor = lax.rsqrt(lax.optimization_barrier(jnp.mean(values32 * values32, axis=-1, keepdims=True)) + 1e-06)
    return (values32 * factor * gain).astype(jnp.bfloat16)

def attend(query_rows, key_block, value_block, counts):
    units = query_rows.shape[0]
    tile_rows = query_rows.shape[1]
    key_flat = key_block.reshape(units, -1, key_block.shape[-1]).astype(jnp.float32)
    value_flat = value_block.reshape(units, -1, value_block.shape[-1]).astype(jnp.float32)
    scores = jnp.einsum('uqd,ukd->uqk', query_rows.astype(jnp.float32), key_flat) / math.sqrt(query_rows.shape[-1])
    list_place = jnp.arange(key_flat.shape[1]) // tile_rows
    valid = (list_place[None, :] < counts[:, None])[:, None, :]
    masked = jnp.where(valid, scores, -jnp.inf)
    peak = lax.optimization_barrier(jnp.max(masked, axis=-1, keepdims=True))
    weights = jnp.where(valid, jnp.exp(masked - peak), jnp.float32(0.0))
    total = lax.optimization_barrier(jnp.sum(weights, axis=-1, keepdims=True))
    probs = weights.astype(jnp.bfloat16)
    mixed = jnp.einsum('uqk,ukd->uqd', probs.astype(jnp.float32), value_flat) / total
    return mixed.astype(jnp.bfloat16)

def reference(queries, keys, values, q_gain, k_gain, key_tiles, key_count):
    q_split = normed(queries, q_gain).reshape(TILES, TILE, HEADS, HEAD_DIM).transpose(2, 0, 1, 3)
    k_split = normed(keys, k_gain).reshape(TILES, TILE, HEADS, HEAD_DIM).transpose(2, 0, 1, 3)
    v_split = values.reshape(TILES, TILE, HEADS, HEAD_DIM).transpose(2, 0, 1, 3)

    def per_head(head_items):
        q_head, k_head, v_head, key_lists, counts = head_items
        return attend(q_head, k_head[key_lists], v_head[key_lists], counts)
    result = lax.map(per_head, (q_split, k_split, v_split, key_tiles, key_count))
    return result.transpose(1, 2, 0, 3).reshape(TOKENS, D)
```

```python
import functools
import math

import jax
import jax.numpy as jnp
from jax import lax
from jax.experimental import pallas as pl
from jax.experimental.pallas import tpu as pltpu
from jax.sharding import PartitionSpec as P

HEADS = 40
HEAD_DIM = 128
TILE = 128


group_size = 4


def normed(rows, gain):
    values32 = rows.astype(jnp.float32)
    factor = lax.rsqrt(jnp.mean(values32 * values32, axis=-1, keepdims=True) + 1e-06)
    return (values32 * factor * gain).astype(jnp.bfloat16)


def padded(entries, length):
    return jnp.pad(entries, (0, length - entries.shape[0]), mode="edge")


def attend_units(received, slot_index, tile_index, head_index, key_tiles, key_count):

    def one_group(unit_items):
        slot_part, tile_part, head_part = unit_items
        query_rows = received[tile_part, slot_part, 0]
        key_lists = key_tiles[head_part, tile_part]
        counts = key_count[head_part, tile_part]
        key_block = received[key_lists, slot_part[:, None], 1]
        value_block = received[key_lists, slot_part[:, None], 2]
        units = query_rows.shape[0]
        tile_rows = query_rows.shape[1]
        key_flat = key_block.reshape(units, -1, key_block.shape[-1])
        value_flat = value_block.reshape(units, -1, value_block.shape[-1])
        scores = jnp.einsum(
            "uqd,ukd->uqk", query_rows, key_flat, preferred_element_type=jnp.float32
        ) / math.sqrt(query_rows.shape[-1])
        list_place = jnp.arange(key_flat.shape[1]) // tile_rows
        valid = (list_place[None, :] < counts[:, None])[:, None, :]
        masked = jnp.where(valid, scores, -jnp.inf)
        peak = jnp.max(masked, axis=-1, keepdims=True)
        weights = jnp.where(valid, jnp.exp(masked - peak), jnp.float32(0.0))
        total = jnp.sum(weights, axis=-1, keepdims=True)
        probs = weights.astype(jnp.bfloat16)
        mixed = (
            jnp.einsum("uqk,ukd->uqd", probs, value_flat, preferred_element_type=jnp.float32)
            / total
        )
        return mixed.astype(jnp.bfloat16)

    grouped = (
        slot_index.reshape(-1, group_size),
        tile_index.reshape(-1, group_size),
        head_index.reshape(-1, group_size),
    )
    result = lax.map(one_group, grouped)
    return result.reshape(-1, result.shape[2], result.shape[3])


def exchanged(queries, keys, values, q_gain, k_gain, key_tiles, key_count):
    devices = lax.axis_size("seq")
    my_index = lax.axis_index("seq")
    q_normed = normed(queries, q_gain)
    k_normed = normed(keys, k_gain)
    stacked = (
        jnp.stack([q_normed, k_normed, values])
        .reshape(3, TILE, HEADS, HEAD_DIM)
        .transpose(2, 0, 1, 3)
    )
    targets = jnp.arange(devices)
    per_device = (HEADS + devices - 1) // devices
    total_slots = devices * per_device
    fewest_slots = total_slots // HEADS
    most_units = (devices + fewest_slots - 1) // fewest_slots

    def slot_layout(slot_number):
        head_of = slot_number * HEADS // total_slots
        head_start = (head_of * total_slots + HEADS - 1) // HEADS
        head_end = ((head_of + 1) * total_slots + HEADS - 1) // HEADS
        sharers = head_end - head_start
        within = slot_number - head_start
        return (head_of, within * devices // sharers, (within + 1) * devices // sharers)

    all_slots = jnp.arange(total_slots).reshape(devices, per_device)
    send_heads = slot_layout(all_slots)[0]
    received = lax.all_to_all(stacked[send_heads], "seq", split_axis=0, concat_axis=0, tiled=True)
    own_heads, lower_tile, upper_tile = slot_layout(my_index * per_device + jnp.arange(per_device))
    offsets = jnp.arange(most_units)
    tile_grid = jnp.minimum(lower_tile[:, None] + offsets[None, :], devices - 1)
    slot_grid = jnp.broadcast_to(jnp.arange(per_device)[:, None], tile_grid.shape)
    head_grid = jnp.broadcast_to(own_heads[:, None], tile_grid.shape)
    unit_total = per_device * most_units
    length = (unit_total + group_size - 1) // group_size * group_size
    finished = attend_units(
        received,
        padded(slot_grid.reshape(-1), length),
        padded(tile_grid.reshape(-1), length),
        padded(head_grid.reshape(-1), length),
        key_tiles,
        key_count,
    )[:unit_total]
    finished = finished.reshape(per_device, most_units, TILE, HEAD_DIM)
    position = targets[:, None] - lower_tile[None, :]
    inside = (position >= 0) & (targets[:, None] < upper_tile[None, :])
    gathered = finished[jnp.arange(per_device)[None, :], jnp.clip(position, 0, most_units - 1)]
    outgoing = jnp.where(inside[:, :, None, None], gathered, jnp.zeros_like(gathered))
    returned = lax.all_to_all(outgoing, "seq", split_axis=0, concat_axis=0, tiled=True)
    head_list = jnp.arange(HEADS)
    head_start = (head_list * total_slots + HEADS - 1) // HEADS
    sharers = ((head_list + 1) * total_slots + HEADS - 1) // HEADS - head_start
    owner_slot = head_start + ((my_index + 1) * sharers - 1) // devices
    pieces = returned[owner_slot // per_device, owner_slot % per_device]
    return pieces.transpose(1, 0, 2).reshape(TILE, HEADS * HEAD_DIM)


CHUNK = 4
ROWS = 16


def fused_kernel(
    devices,
    per_chip,
    tiles_hbm,
    count_hbm,
    q_hbm,
    k_hbm,
    qg_hbm,
    kg_hbm,
    v_ref,
    out_ref,
    qk_out,
    done_buf,
    score_buf,
    qk_send,
    v_send,
    o_send,
    qk_recv,
    v_recv,
    o_recv,
    loads,
    tiles_ref,
    count_ref,
    q_ref,
    k_ref,
    qg_ref,
    kg_ref,
    *landing,
):
    me = lax.axis_index("seq")
    first = (per_chip + 1) // 2
    second = per_chip - first
    qk_in, v_in = landing[:first], landing[first:]
    keep = tiles_ref.shape[1]
    scale = math.log2(math.e) / math.sqrt(HEAD_DIM)

    def slots_of(device):
        return first - lax.rem(device, 2) * (first - second)

    def head_of(device, slot):
        return (device // 2) * per_chip + lax.rem(device, 2) * first + slot

    def columns(head):
        return pl.ds(pl.multiple_of(head * HEAD_DIM, HEAD_DIM), HEAD_DIM)

    load_q = pltpu.make_async_copy(q_hbm, q_ref, loads.at[0])
    load_k = pltpu.make_async_copy(k_hbm, k_ref, loads.at[1])
    load_tiles = pltpu.make_async_copy(tiles_hbm, tiles_ref, loads.at[2])
    load_count = pltpu.make_async_copy(count_hbm, count_ref, loads.at[3])
    load_qg = pltpu.make_async_copy(qg_hbm, qg_ref, loads.at[4])
    load_kg = pltpu.make_async_copy(kg_hbm, kg_ref, loads.at[5])
    barrier = pltpu.get_barrier_semaphore()

    @pl.loop(1, devices)
    def _(step):
        pl.semaphore_signal(barrier, inc=1, device_id={"seq": lax.rem(me + step, devices)})

    load_qg.start()
    load_kg.start()
    load_q.start()
    load_k.start()
    load_tiles.start()
    load_count.start()
    pl.semaphore_wait(barrier, devices - 1)

    def v_copy(head, slot, device):
        return pltpu.make_async_remote_copy(
            src_ref=v_ref.at[:, columns(head)],
            dst_ref=v_in[slot].at[me],
            send_sem=v_send,
            recv_sem=v_recv.at[slot],
            device_id={"seq": device},
        )

    def qk_copy(head, slot, device):
        return pltpu.make_async_remote_copy(
            src_ref=qk_out.at[head],
            dst_ref=qk_in[slot].at[me],
            send_sem=qk_send,
            recv_sem=qk_recv.at[slot],
            device_id={"seq": device},
        )

    def own_v(head, slot):
        return pltpu.make_async_copy(v_ref.at[:, columns(head)], v_in[slot].at[me], v_recv.at[slot])

    def own_qk(head, slot):
        return pltpu.make_async_copy(qk_out.at[head], qk_in[slot].at[me], qk_recv.at[slot])

    half_size = devices // 2
    my_half = me // half_size

    def send_slot(remote, own, slot):
        @pl.loop(0, devices)
        def _(step):
            half = lax.rem(my_half + 1 + step, 2)
            device = half * half_size + lax.rem(me + step // 2, half_size)
            head = head_of(device, slot)
            there = slot < slots_of(device)

            @pl.when(jnp.logical_and(there, device != me))
            def _():
                remote(head, slot, device).start()

            @pl.when(jnp.logical_and(there, device == me))
            def _():
                own(head, slot).start()

    def send_all(remote, own):
        for slot in range(first):
            send_slot(remote, own, slot)

    send_all(v_copy, own_v)

    def norm_into(rows_ref, gain_ref, which):
        @pl.loop(0, TILE // ROWS)
        def _(block):
            rows = pl.ds(pl.multiple_of(block * ROWS, ROWS), ROWS)
            wide = rows_ref[rows, :].astype(jnp.float32)
            factor = lax.rsqrt(jnp.mean(wide * wide, axis=-1, keepdims=True) + 1e-06)
            for head in range(HEADS):
                part = slice(head * HEAD_DIM, (head + 1) * HEAD_DIM)
                qk_out[head, which, rows, :] = (wide[:, part] * factor * gain_ref[:, part]).astype(
                    jnp.bfloat16
                )

    load_qg.wait()
    load_kg.wait()
    load_q.wait()
    norm_into(q_ref, qg_ref, 0)
    load_k.wait()
    norm_into(k_ref, kg_ref, 1)
    send_all(qk_copy, own_qk)
    load_tiles.wait()
    load_count.wait()

    def o_copy(slot, tile):
        return pltpu.make_async_remote_copy(
            src_ref=done_buf.at[slot, tile],
            dst_ref=out_ref.at[:, columns(head_of(me, slot))],
            send_sem=o_send,
            recv_sem=o_recv,
            device_id={"seq": tile},
        )

    def unit(slot, tile, half):
        head = head_of(me, slot)
        query = qk_in[slot][tile, 0]
        count = count_ref[tile, head]
        entries = [tiles_ref[tile, place, head] for place in range(keep)]
        peak = None
        for start in range(0, keep, CHUNK):
            places = range(start, start + CHUNK)
            block = jnp.concatenate([qk_in[slot][entries[place], 1] for place in places], axis=0)
            scores = lax.dot_general(
                query, block, (((1,), (1,)), ((), ())), preferred_element_type=jnp.float32
            )
            for place in places:
                at = (place - start) * TILE
                bias = jnp.where(place < count, jnp.float32(0.0), jnp.float32(-jnp.inf))
                piece = scores[:, at : at + TILE] + bias
                score_buf[half, :, place * TILE : (place + 1) * TILE] = piece
                peak = piece if peak is None else jnp.maximum(peak, piece)
        peak = jnp.max(peak, axis=-1, keepdims=True)
        total = None
        mixed = None
        for start in range(0, keep, CHUNK):
            places = range(start, start + CHUNK)
            probs = []
            for place in places:
                weights = jnp.exp2(
                    (score_buf[half, :, place * TILE : (place + 1) * TILE] - peak) * scale
                )
                total = weights if total is None else total + weights
                probs.append(weights.astype(jnp.bfloat16))
            block = jnp.concatenate([v_in[slot][entries[place]] for place in places], axis=0)
            term = jnp.dot(
                jnp.concatenate(probs, axis=1), block, preferred_element_type=jnp.float32
            )
            mixed = term if mixed is None else mixed + term
        total = jnp.sum(total, axis=-1, keepdims=True)
        done_buf[slot, tile] = (mixed / total).astype(jnp.bfloat16)

    def attend_slot(slot):
        pltpu.make_async_copy(v_in[slot], v_in[slot], v_recv.at[slot]).wait()
        pltpu.make_async_copy(qk_in[slot], qk_in[slot], qk_recv.at[slot]).wait()

        @pl.loop(0, devices // 2)
        def _(pair):
            quarter = devices // 4
            order = pair // quarter * quarter + lax.rem(me + pair, quarter)
            tiles = [(1 - my_half) * half_size + order, my_half * half_size + order]
            for half in range(2):
                unit(slot, tiles[half], half)
            for half in range(2):
                tile = tiles[half]

                @pl.when(tile != me)
                def _():
                    o_copy(slot, tile).start()

                @pl.when(tile == me)
                def _():
                    pltpu.make_async_copy(
                        done_buf.at[slot, tile], out_ref.at[:, columns(head_of(me, slot))], o_recv
                    ).start()

    for slot in range(first):
        pl.when(slot < slots_of(me))(functools.partial(attend_slot, slot))

    def wait_sends(mine):
        away = HEADS - mine
        pltpu.make_async_copy(
            qk_out.at[pl.ds(0, away), 0], qk_out.at[pl.ds(0, away), 0], v_send
        ).wait()
        pltpu.make_async_copy(qk_out.at[pl.ds(0, away)], qk_out.at[pl.ds(0, away)], qk_send).wait()
        sent = done_buf.at[pl.ds(0, mine), pl.ds(0, devices - 1)]
        pltpu.make_async_copy(sent, sent, o_send).wait()

    core = lax.rem(me, 2)
    pl.when(core == 0)(lambda: wait_sends(first))
    pl.when(core == 1)(lambda: wait_sends(second))
    pltpu.make_async_copy(out_ref, out_ref, o_recv).wait()


def fused(queries, keys, values, q_gain, k_gain, key_tiles, key_count):
    devices = lax.axis_size("seq")
    per_chip = HEADS // (devices // 2)
    slots = (per_chip + 1) // 2
    block = (TILE, HEAD_DIM)
    tiles = key_tiles.transpose(1, 2, 0)
    counts = key_count.transpose(1, 0)
    return pl.pallas_call(
        functools.partial(fused_kernel, devices, per_chip),
        out_shape=jax.ShapeDtypeStruct(queries.shape, jnp.bfloat16),
        in_specs=[pl.BlockSpec(memory_space=pl.ANY)] * 7,
        out_specs=pl.BlockSpec(memory_space=pl.ANY),
        scratch_shapes=[
            pltpu.VMEM((HEADS, 2) + block, jnp.bfloat16),
            pltpu.VMEM((slots, devices) + block, jnp.bfloat16),
            pltpu.VMEM((2, TILE, key_tiles.shape[2] * TILE), jnp.float32),
            pltpu.SemaphoreType.DMA,
            pltpu.SemaphoreType.DMA,
            pltpu.SemaphoreType.DMA,
            pltpu.SemaphoreType.DMA((slots,)),
            pltpu.SemaphoreType.DMA((slots,)),
            pltpu.SemaphoreType.DMA,
            pltpu.SemaphoreType.DMA((6,)),
            pltpu.SMEM(tiles.shape, jnp.int32),
            pltpu.SMEM(counts.shape, jnp.int32),
            pltpu.VMEM(queries.shape, jnp.bfloat16),
            pltpu.VMEM(keys.shape, jnp.bfloat16),
            pltpu.VMEM((1, q_gain.shape[0]), jnp.float32),
            pltpu.VMEM((1, k_gain.shape[0]), jnp.float32),
        ]
        + [pltpu.VMEM((devices, 2) + block, jnp.bfloat16)] * slots
        + [pltpu.VMEM((devices,) + block, jnp.bfloat16)] * slots,
        compiler_params=pltpu.CompilerParams(
            collective_id=0, has_side_effects=True, vmem_limit_bytes=24000 * 1024
        ),
    )(
        *[
            pltpu.with_memory_space_constraint(array, pltpu.HBM)
            for array in (
                tiles,
                counts,
                queries,
                keys,
                q_gain.reshape(1, -1),
                k_gain.reshape(1, -1),
                values,
            )
        ]
    )


def local(queries, keys, values, q_gain, k_gain, key_tiles, key_count):
    devices = lax.axis_size("seq")
    whole_heads = devices % 2 == 0 and HEADS % (devices // 2) == 0 and 2 * HEADS >= 2 * devices
    if whole_heads and queries.shape[0] == TILE and key_tiles.shape[2] % CHUNK == 0:
        return fused(queries, keys, values, q_gain, k_gain, key_tiles, key_count)
    return exchanged(queries, keys, values, q_gain, k_gain, key_tiles, key_count)


def solution(mesh):
    in_specs = (
        P(("groups", "seq"), None),
        P(("groups", "seq"), None),
        P(("groups", "seq"), None),
        P(),
        P(),
        P(),
        P(),
    )
    out_specs = P(("groups", "seq"), None)
    return jax.shard_map(local, mesh=mesh, in_specs=in_specs, out_specs=out_specs, check_vma=False)
```

```python
import functools
import math

import jax
import jax.numpy as jnp
from jax import lax
from jax.experimental import pallas as pl
from jax.experimental.pallas import tpu as pltpu
from jax.sharding import PartitionSpec as P

HEADS = 40
HEAD_DIM = 128
TILE = 128


group_size = 4


def normed(rows, gain):
    values32 = rows.astype(jnp.float32)
    factor = lax.rsqrt(jnp.mean(values32 * values32, axis=-1, keepdims=True) + 1e-06)
    return (values32 * factor * gain).astype(jnp.bfloat16)


def padded(entries, length):
    return jnp.pad(entries, (0, length - entries.shape[0]), mode="edge")


def attend_units(received, slot_index, tile_index, head_index, key_tiles, key_count):

    def one_group(unit_items):
        slot_part, tile_part, head_part = unit_items
        query_rows = received[tile_part, slot_part, 0]
        key_lists = key_tiles[head_part, tile_part]
        counts = key_count[head_part, tile_part]
        key_block = received[key_lists, slot_part[:, None], 1]
        value_block = received[key_lists, slot_part[:, None], 2]
        units = query_rows.shape[0]
        tile_rows = query_rows.shape[1]
        key_flat = key_block.reshape(units, -1, key_block.shape[-1])
        value_flat = value_block.reshape(units, -1, value_block.shape[-1])
        scores = jnp.einsum(
            "uqd,ukd->uqk", query_rows, key_flat, preferred_element_type=jnp.float32
        ) / math.sqrt(query_rows.shape[-1])
        list_place = jnp.arange(key_flat.shape[1]) // tile_rows
        valid = (list_place[None, :] < counts[:, None])[:, None, :]
        masked = jnp.where(valid, scores, -jnp.inf)
        peak = jnp.max(masked, axis=-1, keepdims=True)
        weights = jnp.where(valid, jnp.exp(masked - peak), jnp.float32(0.0))
        total = jnp.sum(weights, axis=-1, keepdims=True)
        probs = weights.astype(jnp.bfloat16)
        mixed = (
            jnp.einsum("uqk,ukd->uqd", probs, value_flat, preferred_element_type=jnp.float32)
            / total
        )
        return mixed.astype(jnp.bfloat16)

    grouped = (
        slot_index.reshape(-1, group_size),
        tile_index.reshape(-1, group_size),
        head_index.reshape(-1, group_size),
    )
    result = lax.map(one_group, grouped)
    return result.reshape(-1, result.shape[2], result.shape[3])


def exchanged(queries, keys, values, q_gain, k_gain, key_tiles, key_count):
    devices = lax.axis_size("seq")
    my_index = lax.axis_index("seq")
    q_normed = normed(queries, q_gain)
    k_normed = normed(keys, k_gain)
    stacked = (
        jnp.stack([q_normed, k_normed, values])
        .reshape(3, TILE, HEADS, HEAD_DIM)
        .transpose(2, 0, 1, 3)
    )
    targets = jnp.arange(devices)
    per_device = (HEADS + devices - 1) // devices
    total_slots = devices * per_device
    fewest_slots = total_slots // HEADS
    most_units = (devices + fewest_slots - 1) // fewest_slots

    def slot_layout(slot_number):
        head_of = slot_number * HEADS // total_slots
        head_start = (head_of * total_slots + HEADS - 1) // HEADS
        head_end = ((head_of + 1) * total_slots + HEADS - 1) // HEADS
        sharers = head_end - head_start
        within = slot_number - head_start
        return (head_of, within * devices // sharers, (within + 1) * devices // sharers)

    all_slots = jnp.arange(total_slots).reshape(devices, per_device)
    send_heads = slot_layout(all_slots)[0]
    received = lax.all_to_all(stacked[send_heads], "seq", split_axis=0, concat_axis=0, tiled=True)
    own_heads, lower_tile, upper_tile = slot_layout(my_index * per_device + jnp.arange(per_device))
    offsets = jnp.arange(most_units)
    tile_grid = jnp.minimum(lower_tile[:, None] + offsets[None, :], devices - 1)
    slot_grid = jnp.broadcast_to(jnp.arange(per_device)[:, None], tile_grid.shape)
    head_grid = jnp.broadcast_to(own_heads[:, None], tile_grid.shape)
    unit_total = per_device * most_units
    length = (unit_total + group_size - 1) // group_size * group_size
    finished = attend_units(
        received,
        padded(slot_grid.reshape(-1), length),
        padded(tile_grid.reshape(-1), length),
        padded(head_grid.reshape(-1), length),
        key_tiles,
        key_count,
    )[:unit_total]
    finished = finished.reshape(per_device, most_units, TILE, HEAD_DIM)
    position = targets[:, None] - lower_tile[None, :]
    inside = (position >= 0) & (targets[:, None] < upper_tile[None, :])
    gathered = finished[jnp.arange(per_device)[None, :], jnp.clip(position, 0, most_units - 1)]
    outgoing = jnp.where(inside[:, :, None, None], gathered, jnp.zeros_like(gathered))
    returned = lax.all_to_all(outgoing, "seq", split_axis=0, concat_axis=0, tiled=True)
    head_list = jnp.arange(HEADS)
    head_start = (head_list * total_slots + HEADS - 1) // HEADS
    sharers = ((head_list + 1) * total_slots + HEADS - 1) // HEADS - head_start
    owner_slot = head_start + ((my_index + 1) * sharers - 1) // devices
    pieces = returned[owner_slot // per_device, owner_slot % per_device]
    return pieces.transpose(1, 0, 2).reshape(TILE, HEADS * HEAD_DIM)


CHUNK = 4
ROWS = 16


def fused_kernel(
    devices,
    per_chip,
    tiles_hbm,
    count_hbm,
    q_hbm,
    k_hbm,
    qg_hbm,
    kg_hbm,
    v_ref,
    out_ref,
    qk_out,
    done_buf,
    score_buf,
    qk_send,
    v_send,
    o_send,
    qk_recv,
    v_recv,
    o_recv,
    loads,
    outer_in,
    all_in,
    tiles_ref,
    count_ref,
    q_ref,
    k_ref,
    qg_ref,
    kg_ref,
    *landing,
):
    me = lax.axis_index("seq")
    first = (per_chip + 1) // 2
    second = per_chip - first
    qk_in, v_in = landing[:first], landing[first:]
    keep = tiles_ref.shape[1]
    scale = math.log2(math.e) / math.sqrt(HEAD_DIM)

    def slots_of(device):
        return first - lax.rem(device, 2) * (first - second)

    def head_of(device, slot):
        return (device // 2) * per_chip + lax.rem(device, 2) * first + slot

    def columns(head):
        return pl.ds(pl.multiple_of(head * HEAD_DIM, HEAD_DIM), HEAD_DIM)

    load_q = pltpu.make_async_copy(q_hbm, q_ref, loads.at[0])
    load_k = pltpu.make_async_copy(k_hbm, k_ref, loads.at[1])
    load_tiles = pltpu.make_async_copy(tiles_hbm, tiles_ref, loads.at[2])
    load_count = pltpu.make_async_copy(count_hbm, count_ref, loads.at[3])
    load_qg = pltpu.make_async_copy(qg_hbm, qg_ref, loads.at[4])
    load_kg = pltpu.make_async_copy(kg_hbm, kg_ref, loads.at[5])
    barrier = pltpu.get_barrier_semaphore()
    half_size = devices // 2
    quarter = devices // 4
    my_half = me // half_size
    middle = jnp.logical_and(me >= quarter, me < devices - quarter)

    @pl.when(middle)
    def _():
        @pl.loop(1, devices)
        def _(step):
            pl.semaphore_signal(barrier, inc=1, device_id={"seq": lax.rem(me + step, devices)})

    load_qg.start()
    load_kg.start()
    load_q.start()
    load_k.start()
    load_tiles.start()
    load_count.start()
    pl.semaphore_wait(barrier, half_size - middle.astype(jnp.int32))

    @pl.when(jnp.logical_not(middle))
    def _():
        @pl.loop(0, half_size)
        def _(step):
            pl.semaphore_signal(
                outer_in, inc=1, device_id={"seq": quarter + lax.rem(me + step, half_size)}
            )


    def v_copy(head, slot, device):
        return pltpu.make_async_remote_copy(
            src_ref=v_ref.at[:, columns(head)],
            dst_ref=v_in[slot].at[me],
            send_sem=v_send,
            recv_sem=v_recv.at[slot],
            device_id={"seq": device},
        )

    def qk_copy(head, slot, device):
        return pltpu.make_async_remote_copy(
            src_ref=qk_out.at[head],
            dst_ref=qk_in[slot].at[me],
            send_sem=qk_send,
            recv_sem=qk_recv.at[slot],
            device_id={"seq": device},
        )

    def own_v(head, slot):
        return pltpu.make_async_copy(v_ref.at[:, columns(head)], v_in[slot].at[me], v_recv.at[slot])

    def own_qk(head, slot):
        return pltpu.make_async_copy(qk_out.at[head], qk_in[slot].at[me], qk_recv.at[slot])

    def send_slot(remote, own, slot, device_at, steps):
        @pl.loop(0, steps)
        def _(step):
            half = lax.rem(my_half + 1 + step, 2)
            device = device_at(half, step // 2)
            head = head_of(device, slot)
            there = slot < slots_of(device)

            @pl.when(jnp.logical_and(there, device != me))
            def _():
                remote(head, slot, device).start()

            @pl.when(jnp.logical_and(there, device == me))
            def _():
                own(head, slot).start()

    def any_device(half, step):
        return half * half_size + lax.rem(me + step, half_size)

    def middle_device(half, step):
        return quarter + half * quarter + lax.rem(me + step, quarter)

    def outer_device(half, step):
        return half * (devices - quarter) + lax.rem(me + step, quarter)

    def send_all(remote, own, device_at, steps):
        for slot in range(first):
            send_slot(remote, own, slot, device_at, steps)

    send_all(v_copy, own_v, middle_device, half_size)

    @pl.when(middle)
    def _():
        pl.semaphore_wait(outer_in, half_size)
        pl.semaphore_signal(
            all_in, inc=1, device_id={"seq": me + (2 * my_half - 1) * quarter}
        )

    @pl.when(jnp.logical_not(middle))
    def _():
        pl.semaphore_wait(all_in, 1)

    send_all(v_copy, own_v, outer_device, half_size)

    def norm_into(rows_ref, gain_ref, which):
        @pl.loop(0, TILE // ROWS)
        def _(block):
            rows = pl.ds(pl.multiple_of(block * ROWS, ROWS), ROWS)
            wide = rows_ref[rows, :].astype(jnp.float32)
            factor = lax.rsqrt(jnp.mean(wide * wide, axis=-1, keepdims=True) + 1e-06)
            for head in range(HEADS):
                part = slice(head * HEAD_DIM, (head + 1) * HEAD_DIM)
                qk_out[head, which, rows, :] = (wide[:, part] * factor * gain_ref[:, part]).astype(
                    jnp.bfloat16
                )

    load_qg.wait()
    load_kg.wait()
    load_q.wait()
    norm_into(q_ref, qg_ref, 0)
    load_k.wait()
    norm_into(k_ref, kg_ref, 1)
    send_all(qk_copy, own_qk, any_device, devices)
    load_tiles.wait()
    load_count.wait()

    def o_copy(slot, tile):
        return pltpu.make_async_remote_copy(
            src_ref=done_buf.at[slot, tile],
            dst_ref=out_ref.at[:, columns(head_of(me, slot))],
            send_sem=o_send,
            recv_sem=o_recv,
            device_id={"seq": tile},
        )

    def unit(slot, tile, half):
        head = head_of(me, slot)
        query = qk_in[slot][tile, 0]
        count = count_ref[tile, head]
        entries = [tiles_ref[tile, place, head] for place in range(keep)]
        peak = None
        for start in range(0, keep, CHUNK):
            places = range(start, start + CHUNK)
            block = jnp.concatenate([qk_in[slot][entries[place], 1] for place in places], axis=0)
            scores = lax.dot_general(
                query, block, (((1,), (1,)), ((), ())), preferred_element_type=jnp.float32
            )
            for place in places:
                at = (place - start) * TILE
                bias = jnp.where(place < count, jnp.float32(0.0), jnp.float32(-jnp.inf))
                piece = scores[:, at : at + TILE] + bias
                score_buf[half, :, place * TILE : (place + 1) * TILE] = piece
                peak = piece if peak is None else jnp.maximum(peak, piece)
        peak = jnp.max(peak, axis=-1, keepdims=True)
        total = None
        mixed = None
        for start in range(0, keep, CHUNK):
            places = range(start, start + CHUNK)
            probs = []
            for place in places:
                weights = jnp.exp2(
                    (score_buf[half, :, place * TILE : (place + 1) * TILE] - peak) * scale
                )
                total = weights if total is None else total + weights
                probs.append(weights.astype(jnp.bfloat16))
            block = jnp.concatenate([v_in[slot][entries[place]] for place in places], axis=0)
            term = jnp.dot(
                jnp.concatenate(probs, axis=1), block, preferred_element_type=jnp.float32
            )
            mixed = term if mixed is None else mixed + term
        total = jnp.sum(total, axis=-1, keepdims=True)
        done_buf[slot, tile] = (mixed / total).astype(jnp.bfloat16)

    def attend_slot(slot):
        pltpu.make_async_copy(v_in[slot], v_in[slot], v_recv.at[slot]).wait()
        pltpu.make_async_copy(qk_in[slot], qk_in[slot], qk_recv.at[slot]).wait()

        @pl.loop(0, devices // 2)
        def _(pair):
            order = pair // quarter * quarter + lax.rem(me + pair, quarter)
            tiles = [(1 - my_half) * half_size + order, my_half * half_size + order]
            for half in range(2):
                unit(slot, tiles[half], half)
            for half in range(2):
                tile = tiles[half]

                @pl.when(tile != me)
                def _():
                    o_copy(slot, tile).start()

                @pl.when(tile == me)
                def _():
                    pltpu.make_async_copy(
                        done_buf.at[slot, tile], out_ref.at[:, columns(head_of(me, slot))], o_recv
                    ).start()

    for slot in range(first):
        pl.when(slot < slots_of(me))(functools.partial(attend_slot, slot))

    def wait_sends(mine):
        away = HEADS - mine
        pltpu.make_async_copy(
            qk_out.at[pl.ds(0, away), 0], qk_out.at[pl.ds(0, away), 0], v_send
        ).wait()
        pltpu.make_async_copy(qk_out.at[pl.ds(0, away)], qk_out.at[pl.ds(0, away)], qk_send).wait()
        sent = done_buf.at[pl.ds(0, mine), pl.ds(0, devices - 1)]
        pltpu.make_async_copy(sent, sent, o_send).wait()

    core = lax.rem(me, 2)
    pl.when(core == 0)(lambda: wait_sends(first))
    pl.when(core == 1)(lambda: wait_sends(second))
    pltpu.make_async_copy(out_ref, out_ref, o_recv).wait()


def fused(queries, keys, values, q_gain, k_gain, key_tiles, key_count):
    devices = lax.axis_size("seq")
    per_chip = HEADS // (devices // 2)
    slots = (per_chip + 1) // 2
    block = (TILE, HEAD_DIM)
    tiles = key_tiles.transpose(1, 2, 0)
    counts = key_count.transpose(1, 0)
    return pl.pallas_call(
        functools.partial(fused_kernel, devices, per_chip),
        out_shape=jax.ShapeDtypeStruct(queries.shape, jnp.bfloat16),
        in_specs=[pl.BlockSpec(memory_space=pl.ANY)] * 7,
        out_specs=pl.BlockSpec(memory_space=pl.ANY),
        scratch_shapes=[
            pltpu.VMEM((HEADS, 2) + block, jnp.bfloat16),
            pltpu.VMEM((slots, devices) + block, jnp.bfloat16),
            pltpu.VMEM((2, TILE, key_tiles.shape[2] * TILE), jnp.float32),
            pltpu.SemaphoreType.DMA,
            pltpu.SemaphoreType.DMA,
            pltpu.SemaphoreType.DMA,
            pltpu.SemaphoreType.DMA((slots,)),
            pltpu.SemaphoreType.DMA((slots,)),
            pltpu.SemaphoreType.DMA,
            pltpu.SemaphoreType.DMA((6,)),
            pltpu.SemaphoreType.REGULAR,
            pltpu.SemaphoreType.REGULAR,
            pltpu.SMEM(tiles.shape, jnp.int32),
            pltpu.SMEM(counts.shape, jnp.int32),
            pltpu.VMEM(queries.shape, jnp.bfloat16),
            pltpu.VMEM(keys.shape, jnp.bfloat16),
            pltpu.VMEM((1, q_gain.shape[0]), jnp.float32),
            pltpu.VMEM((1, k_gain.shape[0]), jnp.float32),
        ]
        + [pltpu.VMEM((devices, 2) + block, jnp.bfloat16)] * slots
        + [pltpu.VMEM((devices,) + block, jnp.bfloat16)] * slots,
        compiler_params=pltpu.CompilerParams(
            collective_id=0, has_side_effects=True, vmem_limit_bytes=24000 * 1024
        ),
    )(
        *[
            pltpu.with_memory_space_constraint(array, pltpu.HBM)
            for array in (
                tiles,
                counts,
                queries,
                keys,
                q_gain.reshape(1, -1),
                k_gain.reshape(1, -1),
                values,
            )
        ]
    )


def local(queries, keys, values, q_gain, k_gain, key_tiles, key_count):
    devices = lax.axis_size("seq")
    whole_heads = devices % 4 == 0 and HEADS % (devices // 2) == 0 and 2 * HEADS >= 2 * devices
    if whole_heads and queries.shape[0] == TILE and key_tiles.shape[2] % CHUNK == 0:
        return fused(queries, keys, values, q_gain, k_gain, key_tiles, key_count)
    return exchanged(queries, keys, values, q_gain, k_gain, key_tiles, key_count)


def solution(mesh):
    in_specs = (
        P(("groups", "seq"), None),
        P(("groups", "seq"), None),
        P(("groups", "seq"), None),
        P(),
        P(),
        P(),
        P(),
    )
    out_specs = P(("groups", "seq"), None)
    return jax.shard_map(local, mesh=mesh, in_specs=in_specs, out_specs=out_specs, check_vma=False)
```

```python
import functools
import math

import jax
import jax.numpy as jnp
from jax import lax
from jax.experimental import pallas as pl
from jax.experimental.pallas import tpu as pltpu
from jax.sharding import PartitionSpec as P

HEADS = 40
HEAD_DIM = 128
TILE = 128


group_size = 4


def normed(rows, gain):
    values32 = rows.astype(jnp.float32)
    factor = lax.rsqrt(jnp.mean(values32 * values32, axis=-1, keepdims=True) + 1e-06)
    return (values32 * factor * gain).astype(jnp.bfloat16)


def padded(entries, length):
    return jnp.pad(entries, (0, length - entries.shape[0]), mode="edge")


def attend_units(received, slot_index, tile_index, head_index, key_tiles, key_count):

    def one_group(unit_items):
        slot_part, tile_part, head_part = unit_items
        query_rows = received[tile_part, slot_part, 0]
        key_lists = key_tiles[head_part, tile_part]
        counts = key_count[head_part, tile_part]
        key_block = received[key_lists, slot_part[:, None], 1]
        value_block = received[key_lists, slot_part[:, None], 2]
        units = query_rows.shape[0]
        tile_rows = query_rows.shape[1]
        key_flat = key_block.reshape(units, -1, key_block.shape[-1])
        value_flat = value_block.reshape(units, -1, value_block.shape[-1])
        scores = jnp.einsum(
            "uqd,ukd->uqk", query_rows, key_flat, preferred_element_type=jnp.float32
        ) / math.sqrt(query_rows.shape[-1])
        list_place = jnp.arange(key_flat.shape[1]) // tile_rows
        valid = (list_place[None, :] < counts[:, None])[:, None, :]
        masked = jnp.where(valid, scores, -jnp.inf)
        peak = jnp.max(masked, axis=-1, keepdims=True)
        weights = jnp.where(valid, jnp.exp(masked - peak), jnp.float32(0.0))
        total = jnp.sum(weights, axis=-1, keepdims=True)
        probs = weights.astype(jnp.bfloat16)
        mixed = (
            jnp.einsum("uqk,ukd->uqd", probs, value_flat, preferred_element_type=jnp.float32)
            / total
        )
        return mixed.astype(jnp.bfloat16)

    grouped = (
        slot_index.reshape(-1, group_size),
        tile_index.reshape(-1, group_size),
        head_index.reshape(-1, group_size),
    )
    result = lax.map(one_group, grouped)
    return result.reshape(-1, result.shape[2], result.shape[3])


def exchanged(queries, keys, values, q_gain, k_gain, key_tiles, key_count):
    devices = lax.axis_size("seq")
    my_index = lax.axis_index("seq")
    q_normed = normed(queries, q_gain)
    k_normed = normed(keys, k_gain)
    stacked = (
        jnp.stack([q_normed, k_normed, values])
        .reshape(3, TILE, HEADS, HEAD_DIM)
        .transpose(2, 0, 1, 3)
    )
    targets = jnp.arange(devices)
    per_device = (HEADS + devices - 1) // devices
    total_slots = devices * per_device
    fewest_slots = total_slots // HEADS
    most_units = (devices + fewest_slots - 1) // fewest_slots

    def slot_layout(slot_number):
        head_of = slot_number * HEADS // total_slots
        head_start = (head_of * total_slots + HEADS - 1) // HEADS
        head_end = ((head_of + 1) * total_slots + HEADS - 1) // HEADS
        sharers = head_end - head_start
        within = slot_number - head_start
        return (head_of, within * devices // sharers, (within + 1) * devices // sharers)

    all_slots = jnp.arange(total_slots).reshape(devices, per_device)
    send_heads = slot_layout(all_slots)[0]
    received = lax.all_to_all(stacked[send_heads], "seq", split_axis=0, concat_axis=0, tiled=True)
    own_heads, lower_tile, upper_tile = slot_layout(my_index * per_device + jnp.arange(per_device))
    offsets = jnp.arange(most_units)
    tile_grid = jnp.minimum(lower_tile[:, None] + offsets[None, :], devices - 1)
    slot_grid = jnp.broadcast_to(jnp.arange(per_device)[:, None], tile_grid.shape)
    head_grid = jnp.broadcast_to(own_heads[:, None], tile_grid.shape)
    unit_total = per_device * most_units
    length = (unit_total + group_size - 1) // group_size * group_size
    finished = attend_units(
        received,
        padded(slot_grid.reshape(-1), length),
        padded(tile_grid.reshape(-1), length),
        padded(head_grid.reshape(-1), length),
        key_tiles,
        key_count,
    )[:unit_total]
    finished = finished.reshape(per_device, most_units, TILE, HEAD_DIM)
    position = targets[:, None] - lower_tile[None, :]
    inside = (position >= 0) & (targets[:, None] < upper_tile[None, :])
    gathered = finished[jnp.arange(per_device)[None, :], jnp.clip(position, 0, most_units - 1)]
    outgoing = jnp.where(inside[:, :, None, None], gathered, jnp.zeros_like(gathered))
    returned = lax.all_to_all(outgoing, "seq", split_axis=0, concat_axis=0, tiled=True)
    head_list = jnp.arange(HEADS)
    head_start = (head_list * total_slots + HEADS - 1) // HEADS
    sharers = ((head_list + 1) * total_slots + HEADS - 1) // HEADS - head_start
    owner_slot = head_start + ((my_index + 1) * sharers - 1) // devices
    pieces = returned[owner_slot // per_device, owner_slot % per_device]
    return pieces.transpose(1, 0, 2).reshape(TILE, HEADS * HEAD_DIM)


CHUNK = 4
ROWS = 16


def fused_kernel(
    devices,
    per_chip,
    tiles_hbm,
    count_hbm,
    q_hbm,
    k_hbm,
    qg_hbm,
    kg_hbm,
    v_ref,
    out_ref,
    qk_out,
    done_buf,
    score_buf,
    qk_send,
    v_send,
    o_send,
    qk_recv,
    v_recv,
    o_recv,
    loads,
    outer_in,
    all_in,
    tiles_ref,
    count_ref,
    q_ref,
    k_ref,
    qg_ref,
    kg_ref,
    *landing,
):
    me = lax.axis_index("seq")
    first = (per_chip + 1) // 2
    second = per_chip - first
    qk_in, v_in = landing[:first], landing[first:]
    keep = tiles_ref.shape[1]
    scale = math.log2(math.e) / math.sqrt(HEAD_DIM)

    def slots_of(device):
        return first - lax.rem(device, 2) * (first - second)

    def head_of(device, slot):
        return (device // 2) * per_chip + lax.rem(device, 2) * first + slot

    def columns(head):
        return pl.ds(pl.multiple_of(head * HEAD_DIM, HEAD_DIM), HEAD_DIM)

    load_q = pltpu.make_async_copy(q_hbm, q_ref, loads.at[0])
    load_k = pltpu.make_async_copy(k_hbm, k_ref, loads.at[1])
    load_tiles = pltpu.make_async_copy(tiles_hbm, tiles_ref, loads.at[2])
    load_count = pltpu.make_async_copy(count_hbm, count_ref, loads.at[3])
    load_qg = pltpu.make_async_copy(qg_hbm, qg_ref, loads.at[4])
    load_kg = pltpu.make_async_copy(kg_hbm, kg_ref, loads.at[5])
    barrier = pltpu.get_barrier_semaphore()
    half_size = devices // 2
    quarter = devices // 4
    my_half = me // half_size
    middle = jnp.logical_and(me >= quarter, me < devices - quarter)
    chip = lax.rem(me, quarter) // 2 * 2

    def near_device(half, step):
        return quarter + half * quarter + chip + lax.rem(me + step, 2)

    def outer_device(half, step):
        return half * (devices - quarter) + lax.rem(me + step, quarter)

    @pl.when(middle)
    def _():
        @pl.loop(0, 4)
        def _(step):
            device = near_device(lax.rem(my_half + 1 + step, 2), step // 2)

            @pl.when(device != me)
            def _():
                pl.semaphore_signal(barrier, inc=1, device_id={"seq": device})

        @pl.loop(0, half_size)
        def _(step):
            device = outer_device(lax.rem(my_half + 1 + step, 2), step // 2)
            pl.semaphore_signal(barrier, inc=1, device_id={"seq": device})

    load_qg.start()
    load_kg.start()
    load_q.start()
    load_k.start()
    load_tiles.start()
    load_count.start()
    pl.semaphore_wait(barrier, jnp.where(middle, 3, half_size))

    @pl.when(jnp.logical_not(middle))
    def _():
        @pl.loop(0, half_size)
        def _(step):
            pl.semaphore_signal(
                outer_in, inc=1, device_id={"seq": quarter + lax.rem(me + step, half_size)}
            )

    def v_copy(head, slot, device):
        return pltpu.make_async_remote_copy(
            src_ref=v_ref.at[:, columns(head)],
            dst_ref=v_in[slot].at[me],
            send_sem=v_send,
            recv_sem=v_recv.at[slot],
            device_id={"seq": device},
        )

    def qk_copy(head, slot, device):
        return pltpu.make_async_remote_copy(
            src_ref=qk_out.at[head],
            dst_ref=qk_in[slot].at[me],
            send_sem=qk_send,
            recv_sem=qk_recv.at[slot],
            device_id={"seq": device},
        )

    def own_v(head, slot):
        return pltpu.make_async_copy(v_ref.at[:, columns(head)], v_in[slot].at[me], v_recv.at[slot])

    def own_qk(head, slot):
        return pltpu.make_async_copy(qk_out.at[head], qk_in[slot].at[me], qk_recv.at[slot])

    def send_slot(remote, own, slot, device_at, steps):
        @pl.loop(0, steps)
        def _(step):
            half = lax.rem(my_half + 1 + step, 2)
            device = device_at(half, step // 2)
            head = head_of(device, slot)
            there = slot < slots_of(device)

            @pl.when(jnp.logical_and(there, device != me))
            def _():
                remote(head, slot, device).start()

            @pl.when(jnp.logical_and(there, device == me))
            def _():
                own(head, slot).start()

    def any_device(half, step):
        return half * half_size + lax.rem(me + step, half_size)

    def far_device(half, step):
        place = lax.rem(chip + 2 + step // 2 * 2 + lax.rem(me + step, 2), quarter)
        return quarter + half * quarter + place

    def middle_device(half, step):
        return quarter + half * quarter + lax.rem(me + step, quarter)

    def send_all(remote, own, device_at, steps):
        for slot in range(first):
            send_slot(remote, own, slot, device_at, steps)

    @pl.when(middle)
    def _():
        send_all(v_copy, own_v, near_device, 4)
        pl.semaphore_wait(outer_in, half_size)
        pl.semaphore_signal(
            all_in, inc=1, device_id={"seq": me + (2 * my_half - 1) * quarter}
        )
        send_all(v_copy, own_v, far_device, half_size - 4)

    @pl.when(jnp.logical_not(middle))
    def _():
        send_all(v_copy, own_v, middle_device, half_size)
        pl.semaphore_wait(all_in, 1)

    send_all(v_copy, own_v, outer_device, half_size)

    def norm_into(rows_ref, gain_ref, which):
        @pl.loop(0, TILE // ROWS)
        def _(block):
            rows = pl.ds(pl.multiple_of(block * ROWS, ROWS), ROWS)
            wide = rows_ref[rows, :].astype(jnp.float32)
            factor = lax.rsqrt(jnp.mean(wide * wide, axis=-1, keepdims=True) + 1e-06)
            for head in range(HEADS):
                part = slice(head * HEAD_DIM, (head + 1) * HEAD_DIM)
                qk_out[head, which, rows, :] = (wide[:, part] * factor * gain_ref[:, part]).astype(
                    jnp.bfloat16
                )

    load_qg.wait()
    load_kg.wait()
    load_q.wait()
    norm_into(q_ref, qg_ref, 0)
    load_k.wait()
    norm_into(k_ref, kg_ref, 1)
    send_all(qk_copy, own_qk, any_device, devices)
    load_tiles.wait()
    load_count.wait()

    def o_copy(slot, tile):
        return pltpu.make_async_remote_copy(
            src_ref=done_buf.at[slot, tile],
            dst_ref=out_ref.at[:, columns(head_of(me, slot))],
            send_sem=o_send,
            recv_sem=o_recv,
            device_id={"seq": tile},
        )

    def unit(slot, tile, half):
        head = head_of(me, slot)
        query = qk_in[slot][tile, 0]
        count = count_ref[tile, head]
        entries = [tiles_ref[tile, place, head] for place in range(keep)]
        peak = None
        for start in range(0, keep, CHUNK):
            places = range(start, start + CHUNK)
            block = jnp.concatenate([qk_in[slot][entries[place], 1] for place in places], axis=0)
            scores = lax.dot_general(
                query, block, (((1,), (1,)), ((), ())), preferred_element_type=jnp.float32
            )
            for place in places:
                at = (place - start) * TILE
                bias = jnp.where(place < count, jnp.float32(0.0), jnp.float32(-jnp.inf))
                piece = scores[:, at : at + TILE] + bias
                score_buf[half, :, place * TILE : (place + 1) * TILE] = piece
                peak = piece if peak is None else jnp.maximum(peak, piece)
        peak = jnp.max(peak, axis=-1, keepdims=True)
        total = None
        mixed = None
        for start in range(0, keep, CHUNK):
            places = range(start, start + CHUNK)
            probs = []
            for place in places:
                weights = jnp.exp2(
                    (score_buf[half, :, place * TILE : (place + 1) * TILE] - peak) * scale
                )
                total = weights if total is None else total + weights
                probs.append(weights.astype(jnp.bfloat16))
            block = jnp.concatenate([v_in[slot][entries[place]] for place in places], axis=0)
            term = jnp.dot(
                jnp.concatenate(probs, axis=1), block, preferred_element_type=jnp.float32
            )
            mixed = term if mixed is None else mixed + term
        total = jnp.sum(total, axis=-1, keepdims=True)
        done_buf[slot, tile] = (mixed / total).astype(jnp.bfloat16)

    def attend_slot(slot):
        pltpu.make_async_copy(v_in[slot], v_in[slot], v_recv.at[slot]).wait()
        pltpu.make_async_copy(qk_in[slot], qk_in[slot], qk_recv.at[slot]).wait()

        @pl.loop(0, devices // 2)
        def _(pair):
            order = pair // 2 * 2 + lax.rem(me + pair, 2)
            tiles = [(1 - my_half) * half_size + order, my_half * half_size + order]
            for half in range(2):
                unit(slot, tiles[half], half)
            for half in range(2):
                tile = tiles[half]

                @pl.when(tile != me)
                def _():
                    o_copy(slot, tile).start()

                @pl.when(tile == me)
                def _():
                    pltpu.make_async_copy(
                        done_buf.at[slot, tile], out_ref.at[:, columns(head_of(me, slot))], o_recv
                    ).start()

    for slot in range(first):
        pl.when(slot < slots_of(me))(functools.partial(attend_slot, slot))

    def wait_sends(mine):
        away = HEADS - mine
        pltpu.make_async_copy(
            qk_out.at[pl.ds(0, away), 0], qk_out.at[pl.ds(0, away), 0], v_send
        ).wait()
        pltpu.make_async_copy(qk_out.at[pl.ds(0, away)], qk_out.at[pl.ds(0, away)], qk_send).wait()
        sent = done_buf.at[pl.ds(0, mine), pl.ds(0, devices - 1)]
        pltpu.make_async_copy(sent, sent, o_send).wait()

    core = lax.rem(me, 2)
    pl.when(core == 0)(lambda: wait_sends(first))
    pl.when(core == 1)(lambda: wait_sends(second))
    pltpu.make_async_copy(out_ref, out_ref, o_recv).wait()


def fused(queries, keys, values, q_gain, k_gain, key_tiles, key_count):
    devices = lax.axis_size("seq")
    per_chip = HEADS // (devices // 2)
    slots = (per_chip + 1) // 2
    block = (TILE, HEAD_DIM)
    tiles = key_tiles.transpose(1, 2, 0)
    counts = key_count.transpose(1, 0)
    return pl.pallas_call(
        functools.partial(fused_kernel, devices, per_chip),
        out_shape=jax.ShapeDtypeStruct(queries.shape, jnp.bfloat16),
        in_specs=[pl.BlockSpec(memory_space=pl.ANY)] * 7,
        out_specs=pl.BlockSpec(memory_space=pl.ANY),
        scratch_shapes=[
            pltpu.VMEM((HEADS, 2) + block, jnp.bfloat16),
            pltpu.VMEM((slots, devices) + block, jnp.bfloat16),
            pltpu.VMEM((2, TILE, key_tiles.shape[2] * TILE), jnp.float32),
            pltpu.SemaphoreType.DMA,
            pltpu.SemaphoreType.DMA,
            pltpu.SemaphoreType.DMA,
            pltpu.SemaphoreType.DMA((slots,)),
            pltpu.SemaphoreType.DMA((slots,)),
            pltpu.SemaphoreType.DMA,
            pltpu.SemaphoreType.DMA((6,)),
            pltpu.SemaphoreType.REGULAR,
            pltpu.SemaphoreType.REGULAR,
            pltpu.SMEM(tiles.shape, jnp.int32),
            pltpu.SMEM(counts.shape, jnp.int32),
            pltpu.VMEM(queries.shape, jnp.bfloat16),
            pltpu.VMEM(keys.shape, jnp.bfloat16),
            pltpu.VMEM((1, q_gain.shape[0]), jnp.float32),
            pltpu.VMEM((1, k_gain.shape[0]), jnp.float32),
        ]
        + [pltpu.VMEM((devices, 2) + block, jnp.bfloat16)] * slots
        + [pltpu.VMEM((devices,) + block, jnp.bfloat16)] * slots,
        compiler_params=pltpu.CompilerParams(
            collective_id=0, has_side_effects=True, vmem_limit_bytes=24000 * 1024
        ),
    )(
        *[
            pltpu.with_memory_space_constraint(array, pltpu.HBM)
            for array in (
                tiles,
                counts,
                queries,
                keys,
                q_gain.reshape(1, -1),
                k_gain.reshape(1, -1),
                values,
            )
        ]
    )


def local(queries, keys, values, q_gain, k_gain, key_tiles, key_count):
    devices = lax.axis_size("seq")
    whole_heads = devices % 8 == 0 and HEADS % (devices // 2) == 0 and 2 * HEADS >= 2 * devices
    if whole_heads and queries.shape[0] == TILE and key_tiles.shape[2] % CHUNK == 0:
        return fused(queries, keys, values, q_gain, k_gain, key_tiles, key_count)
    return exchanged(queries, keys, values, q_gain, k_gain, key_tiles, key_count)


def solution(mesh):
    in_specs = (
        P(("groups", "seq"), None),
        P(("groups", "seq"), None),
        P(("groups", "seq"), None),
        P(),
        P(),
        P(),
        P(),
    )
    out_specs = P(("groups", "seq"), None)
    return jax.shard_map(local, mesh=mesh, in_specs=in_specs, out_specs=out_specs, check_vma=False)
```

```python
import functools
import math

import jax
import jax.numpy as jnp
from jax import lax
from jax.experimental import pallas as pl
from jax.experimental.pallas import tpu as pltpu
from jax.sharding import PartitionSpec as P

HEADS = 40
HEAD_DIM = 128
TILE = 128


group_size = 4


def normed(rows, gain):
    values32 = rows.astype(jnp.float32)
    factor = lax.rsqrt(jnp.mean(values32 * values32, axis=-1, keepdims=True) + 1e-06)
    return (values32 * factor * gain).astype(jnp.bfloat16)


def padded(entries, length):
    return jnp.pad(entries, (0, length - entries.shape[0]), mode="edge")


def attend_units(received, slot_index, tile_index, head_index, key_tiles, key_count):

    def one_group(unit_items):
        slot_part, tile_part, head_part = unit_items
        query_rows = received[tile_part, slot_part, 0]
        key_lists = key_tiles[head_part, tile_part]
        counts = key_count[head_part, tile_part]
        key_block = received[key_lists, slot_part[:, None], 1]
        value_block = received[key_lists, slot_part[:, None], 2]
        units = query_rows.shape[0]
        tile_rows = query_rows.shape[1]
        key_flat = key_block.reshape(units, -1, key_block.shape[-1])
        value_flat = value_block.reshape(units, -1, value_block.shape[-1])
        scores = jnp.einsum(
            "uqd,ukd->uqk", query_rows, key_flat, preferred_element_type=jnp.float32
        ) / math.sqrt(query_rows.shape[-1])
        list_place = jnp.arange(key_flat.shape[1]) // tile_rows
        valid = (list_place[None, :] < counts[:, None])[:, None, :]
        masked = jnp.where(valid, scores, -jnp.inf)
        peak = jnp.max(masked, axis=-1, keepdims=True)
        weights = jnp.where(valid, jnp.exp(masked - peak), jnp.float32(0.0))
        total = jnp.sum(weights, axis=-1, keepdims=True)
        probs = weights.astype(jnp.bfloat16)
        mixed = (
            jnp.einsum("uqk,ukd->uqd", probs, value_flat, preferred_element_type=jnp.float32)
            / total
        )
        return mixed.astype(jnp.bfloat16)

    grouped = (
        slot_index.reshape(-1, group_size),
        tile_index.reshape(-1, group_size),
        head_index.reshape(-1, group_size),
    )
    result = lax.map(one_group, grouped)
    return result.reshape(-1, result.shape[2], result.shape[3])


def exchanged(queries, keys, values, q_gain, k_gain, key_tiles, key_count):
    devices = lax.axis_size("seq")
    my_index = lax.axis_index("seq")
    q_normed = normed(queries, q_gain)
    k_normed = normed(keys, k_gain)
    stacked = (
        jnp.stack([q_normed, k_normed, values])
        .reshape(3, TILE, HEADS, HEAD_DIM)
        .transpose(2, 0, 1, 3)
    )
    targets = jnp.arange(devices)
    per_device = (HEADS + devices - 1) // devices
    total_slots = devices * per_device
    fewest_slots = total_slots // HEADS
    most_units = (devices + fewest_slots - 1) // fewest_slots

    def slot_layout(slot_number):
        head_of = slot_number * HEADS // total_slots
        head_start = (head_of * total_slots + HEADS - 1) // HEADS
        head_end = ((head_of + 1) * total_slots + HEADS - 1) // HEADS
        sharers = head_end - head_start
        within = slot_number - head_start
        return (head_of, within * devices // sharers, (within + 1) * devices // sharers)

    all_slots = jnp.arange(total_slots).reshape(devices, per_device)
    send_heads = slot_layout(all_slots)[0]
    received = lax.all_to_all(stacked[send_heads], "seq", split_axis=0, concat_axis=0, tiled=True)
    own_heads, lower_tile, upper_tile = slot_layout(my_index * per_device + jnp.arange(per_device))
    offsets = jnp.arange(most_units)
    tile_grid = jnp.minimum(lower_tile[:, None] + offsets[None, :], devices - 1)
    slot_grid = jnp.broadcast_to(jnp.arange(per_device)[:, None], tile_grid.shape)
    head_grid = jnp.broadcast_to(own_heads[:, None], tile_grid.shape)
    unit_total = per_device * most_units
    length = (unit_total + group_size - 1) // group_size * group_size
    finished = attend_units(
        received,
        padded(slot_grid.reshape(-1), length),
        padded(tile_grid.reshape(-1), length),
        padded(head_grid.reshape(-1), length),
        key_tiles,
        key_count,
    )[:unit_total]
    finished = finished.reshape(per_device, most_units, TILE, HEAD_DIM)
    position = targets[:, None] - lower_tile[None, :]
    inside = (position >= 0) & (targets[:, None] < upper_tile[None, :])
    gathered = finished[jnp.arange(per_device)[None, :], jnp.clip(position, 0, most_units - 1)]
    outgoing = jnp.where(inside[:, :, None, None], gathered, jnp.zeros_like(gathered))
    returned = lax.all_to_all(outgoing, "seq", split_axis=0, concat_axis=0, tiled=True)
    head_list = jnp.arange(HEADS)
    head_start = (head_list * total_slots + HEADS - 1) // HEADS
    sharers = ((head_list + 1) * total_slots + HEADS - 1) // HEADS - head_start
    owner_slot = head_start + ((my_index + 1) * sharers - 1) // devices
    pieces = returned[owner_slot // per_device, owner_slot % per_device]
    return pieces.transpose(1, 0, 2).reshape(TILE, HEADS * HEAD_DIM)


CHUNK = 4
ROWS = 16


def fused_kernel(
    devices,
    per_chip,
    tiles_hbm,
    count_hbm,
    q_hbm,
    k_hbm,
    qg_hbm,
    kg_hbm,
    v_ref,
    out_ref,
    qk_out,
    done_buf,
    score_buf,
    qk_send,
    v_send,
    o_send,
    qk_recv,
    v_recv,
    o_recv,
    loads,
    outer_in,
    all_in,
    tiles_ref,
    count_ref,
    q_ref,
    k_ref,
    qg_ref,
    kg_ref,
    *landing,
):
    me = lax.axis_index("seq")
    first = (per_chip + 1) // 2
    second = per_chip - first
    qk_in, v_in = landing[:first], landing[first:]
    keep = tiles_ref.shape[1]
    scale = math.log2(math.e) / math.sqrt(HEAD_DIM)

    def slots_of(device):
        return first - lax.rem(device, 2) * (first - second)

    def head_of(device, slot):
        return (device // 2) * per_chip + lax.rem(device, 2) * first + slot

    def columns(head):
        return pl.ds(pl.multiple_of(head * HEAD_DIM, HEAD_DIM), HEAD_DIM)

    load_q = pltpu.make_async_copy(q_hbm, q_ref, loads.at[0])
    load_k = pltpu.make_async_copy(k_hbm, k_ref, loads.at[1])
    load_tiles = pltpu.make_async_copy(tiles_hbm, tiles_ref, loads.at[2])
    load_count = pltpu.make_async_copy(count_hbm, count_ref, loads.at[3])
    load_qg = pltpu.make_async_copy(qg_hbm, qg_ref, loads.at[4])
    load_kg = pltpu.make_async_copy(kg_hbm, kg_ref, loads.at[5])
    barrier = pltpu.get_barrier_semaphore()
    half_size = devices // 2
    quarter = devices // 4
    my_half = me // half_size
    middle = jnp.logical_and(me >= quarter, me < devices - quarter)
    chip = lax.rem(me, quarter) // 2 * 2

    def near_device(half, step):
        return quarter + half * quarter + chip + lax.rem(me + step, 2)

    def outer_device(half, step):
        return half * (devices - quarter) + lax.rem(me + step, quarter)

    @pl.when(middle)
    def _():
        @pl.loop(0, 4)
        def _(step):
            device = near_device(lax.rem(my_half + 1 + step, 2), step // 2)

            @pl.when(device != me)
            def _():
                pl.semaphore_signal(barrier, inc=1, device_id={"seq": device})

        @pl.loop(0, half_size)
        def _(step):
            device = outer_device(lax.rem(my_half + 1 + step, 2), step // 2)
            pl.semaphore_signal(barrier, inc=1, device_id={"seq": device})

    load_qg.start()
    load_kg.start()
    load_q.start()
    load_k.start()
    load_tiles.start()
    load_count.start()
    pl.semaphore_wait(barrier, jnp.where(middle, 3, half_size))

    @pl.when(jnp.logical_not(middle))
    def _():
        @pl.loop(0, half_size)
        def _(step):
            pl.semaphore_signal(
                outer_in, inc=1, device_id={"seq": quarter + lax.rem(me + step, half_size)}
            )

    def v_copy(head, slot, device):
        return pltpu.make_async_remote_copy(
            src_ref=v_ref.at[:, columns(head)],
            dst_ref=v_in[slot].at[me],
            send_sem=v_send,
            recv_sem=v_recv.at[slot],
            device_id={"seq": device},
        )

    def qk_copy(head, slot, device):
        return pltpu.make_async_remote_copy(
            src_ref=qk_out.at[head],
            dst_ref=qk_in[slot].at[me],
            send_sem=qk_send,
            recv_sem=qk_recv.at[slot],
            device_id={"seq": device},
        )

    def own_v(head, slot):
        return pltpu.make_async_copy(v_ref.at[:, columns(head)], v_in[slot].at[me], v_recv.at[slot])

    def own_qk(head, slot):
        return pltpu.make_async_copy(qk_out.at[head], qk_in[slot].at[me], qk_recv.at[slot])

    def send_slot(remote, own, slot, device_at, steps):
        @pl.loop(0, steps)
        def _(step):
            half = lax.rem(my_half + 1 + step, 2)
            device = device_at(half, step // 2)
            head = head_of(device, slot)
            there = slot < slots_of(device)

            @pl.when(jnp.logical_and(there, device != me))
            def _():
                remote(head, slot, device).start()

            @pl.when(jnp.logical_and(there, device == me))
            def _():
                own(head, slot).start()

    def any_device(half, step):
        return half * half_size + lax.rem(me + step, half_size)

    def far_device(half, step):
        place = lax.rem(chip + 2 + step // 2 * 2 + lax.rem(me + step, 2), quarter)
        return quarter + half * quarter + place

    def middle_device(half, step):
        return quarter + half * quarter + lax.rem(me + step, quarter)

    def send_all(remote, own, device_at, steps):
        for slot in range(first):
            send_slot(remote, own, slot, device_at, steps)

    @pl.when(middle)
    def _():
        send_all(v_copy, own_v, near_device, 4)
        pl.semaphore_wait(outer_in, half_size)
        pl.semaphore_signal(
            all_in, inc=1, device_id={"seq": me + (2 * my_half - 1) * quarter}
        )
        send_all(v_copy, own_v, far_device, half_size - 4)

    @pl.when(jnp.logical_not(middle))
    def _():
        send_all(v_copy, own_v, middle_device, half_size)
        pl.semaphore_wait(all_in, 1)

    send_all(v_copy, own_v, outer_device, half_size)

    def norm_into(rows_ref, gain_ref, which):
        @pl.loop(0, TILE // ROWS)
        def _(block):
            rows = pl.ds(pl.multiple_of(block * ROWS, ROWS), ROWS)
            wide = rows_ref[rows, :].astype(jnp.float32)
            factor = lax.rsqrt(jnp.mean(wide * wide, axis=-1, keepdims=True) + 1e-06)
            for head in range(HEADS):
                part = slice(head * HEAD_DIM, (head + 1) * HEAD_DIM)
                qk_out[head, which, rows, :] = (wide[:, part] * factor * gain_ref[:, part]).astype(
                    jnp.bfloat16
                )

    load_qg.wait()
    load_kg.wait()
    load_q.wait()
    norm_into(q_ref, qg_ref, 0)
    load_k.wait()
    norm_into(k_ref, kg_ref, 1)
    send_all(qk_copy, own_qk, any_device, devices)
    load_tiles.wait()
    load_count.wait()

    def o_copy(slot, tile):
        return pltpu.make_async_remote_copy(
            src_ref=done_buf.at[slot, tile],
            dst_ref=out_ref.at[:, columns(head_of(me, slot))],
            send_sem=o_send,
            recv_sem=o_recv,
            device_id={"seq": tile},
        )

    def unit(slot, tile, half):
        head = head_of(me, slot)
        query = qk_in[slot][tile, 0]
        count = count_ref[tile, head]
        entries = [tiles_ref[tile, place, head] for place in range(keep)]
        peak = None
        for start in range(0, keep, CHUNK):
            places = range(start, start + CHUNK)
            block = jnp.concatenate([qk_in[slot][entries[place], 1] for place in places], axis=0)
            scores = lax.dot_general(
                query, block, (((1,), (1,)), ((), ())), preferred_element_type=jnp.float32
            )
            for place in places:
                at = (place - start) * TILE
                bias = jnp.where(place < count, jnp.float32(0.0), jnp.float32(-jnp.inf))
                piece = scores[:, at : at + TILE] + bias
                score_buf[half, :, place * TILE : (place + 1) * TILE] = piece
                peak = piece if peak is None else jnp.maximum(peak, piece)
        peak = jnp.max(peak, axis=-1, keepdims=True)
        total = None
        mixed = None
        for start in range(0, keep, CHUNK):
            places = range(start, start + CHUNK)
            probs = []
            for place in places:
                weights = jnp.exp2(
                    (score_buf[half, :, place * TILE : (place + 1) * TILE] - peak) * scale
                )
                total = weights if total is None else total + weights
                probs.append(weights.astype(jnp.bfloat16))
            block = jnp.concatenate([v_in[slot][entries[place]] for place in places], axis=0)
            term = jnp.dot(
                jnp.concatenate(probs, axis=1), block, preferred_element_type=jnp.float32
            )
            mixed = term if mixed is None else mixed + term
        total = jnp.sum(total, axis=-1, keepdims=True)
        done_buf[slot, tile] = (mixed / total).astype(jnp.bfloat16)

    def tiles_at(pair):
        core = 1 - lax.rem(pair, 2)
        return [
            half * half_size + lax.rem(pair // 2 * 2 + half * quarter, half_size) + core
            for half in (1 - my_half, my_half)
        ]

    def return_tiles(slot, pair):
        for tile in tiles_at(pair):

            @pl.when(tile != me)
            def _():
                o_copy(slot, tile).start()

            @pl.when(tile == me)
            def _():
                pltpu.make_async_copy(
                    done_buf.at[slot, tile], out_ref.at[:, columns(head_of(me, slot))], o_recv
                ).start()

    def attend_slot(slot):
        pltpu.make_async_copy(v_in[slot], v_in[slot], v_recv.at[slot]).wait()
        pltpu.make_async_copy(qk_in[slot], qk_in[slot], qk_recv.at[slot]).wait()
        last = slots_of(me) - 1

        @pl.loop(0, devices // 2)
        def _(pair):
            tiles = tiles_at(pair)
            for half in range(2):
                unit(slot, tiles[half], half)
            late = pair >= quarter
            if slot > 0:

                @pl.when(jnp.logical_and(late, slot == last))
                def _():
                    return_tiles(slot - 1, pair)

            @pl.when(jnp.logical_not(jnp.logical_and(late, slot == last - 1)))
            def _():
                return_tiles(slot, pair)

    for slot in range(first):
        pl.when(slot < slots_of(me))(functools.partial(attend_slot, slot))

    def wait_sends(mine):
        away = HEADS - mine
        pltpu.make_async_copy(
            qk_out.at[pl.ds(0, away), 0], qk_out.at[pl.ds(0, away), 0], v_send
        ).wait()
        pltpu.make_async_copy(qk_out.at[pl.ds(0, away)], qk_out.at[pl.ds(0, away)], qk_send).wait()
        sent = done_buf.at[pl.ds(0, mine), pl.ds(0, devices - 1)]
        pltpu.make_async_copy(sent, sent, o_send).wait()

    core = lax.rem(me, 2)
    pl.when(core == 0)(lambda: wait_sends(first))
    pl.when(core == 1)(lambda: wait_sends(second))
    pltpu.make_async_copy(out_ref, out_ref, o_recv).wait()


def fused(queries, keys, values, q_gain, k_gain, key_tiles, key_count):
    devices = lax.axis_size("seq")
    per_chip = HEADS // (devices // 2)
    slots = (per_chip + 1) // 2
    block = (TILE, HEAD_DIM)
    tiles = key_tiles.transpose(1, 2, 0)
    counts = key_count.transpose(1, 0)
    return pl.pallas_call(
        functools.partial(fused_kernel, devices, per_chip),
        out_shape=jax.ShapeDtypeStruct(queries.shape, jnp.bfloat16),
        in_specs=[pl.BlockSpec(memory_space=pl.ANY)] * 7,
        out_specs=pl.BlockSpec(memory_space=pl.ANY),
        scratch_shapes=[
            pltpu.VMEM((HEADS, 2) + block, jnp.bfloat16),
            pltpu.VMEM((slots, devices) + block, jnp.bfloat16),
            pltpu.VMEM((2, TILE, key_tiles.shape[2] * TILE), jnp.float32),
            pltpu.SemaphoreType.DMA,
            pltpu.SemaphoreType.DMA,
            pltpu.SemaphoreType.DMA,
            pltpu.SemaphoreType.DMA((slots,)),
            pltpu.SemaphoreType.DMA((slots,)),
            pltpu.SemaphoreType.DMA,
            pltpu.SemaphoreType.DMA((6,)),
            pltpu.SemaphoreType.REGULAR,
            pltpu.SemaphoreType.REGULAR,
            pltpu.SMEM(tiles.shape, jnp.int32),
            pltpu.SMEM(counts.shape, jnp.int32),
            pltpu.VMEM(queries.shape, jnp.bfloat16),
            pltpu.VMEM(keys.shape, jnp.bfloat16),
            pltpu.VMEM((1, q_gain.shape[0]), jnp.float32),
            pltpu.VMEM((1, k_gain.shape[0]), jnp.float32),
        ]
        + [pltpu.VMEM((devices, 2) + block, jnp.bfloat16)] * slots
        + [pltpu.VMEM((devices,) + block, jnp.bfloat16)] * slots,
        compiler_params=pltpu.CompilerParams(
            collective_id=0, has_side_effects=True, vmem_limit_bytes=24000 * 1024
        ),
    )(
        *[
            pltpu.with_memory_space_constraint(array, pltpu.HBM)
            for array in (
                tiles,
                counts,
                queries,
                keys,
                q_gain.reshape(1, -1),
                k_gain.reshape(1, -1),
                values,
            )
        ]
    )


def local(queries, keys, values, q_gain, k_gain, key_tiles, key_count):
    devices = lax.axis_size("seq")
    whole_heads = devices % 8 == 0 and HEADS % (devices // 2) == 0 and 2 * HEADS >= 2 * devices
    if whole_heads and queries.shape[0] == TILE and key_tiles.shape[2] % CHUNK == 0:
        return fused(queries, keys, values, q_gain, k_gain, key_tiles, key_count)
    return exchanged(queries, keys, values, q_gain, k_gain, key_tiles, key_count)


def solution(mesh):
    in_specs = (
        P(("groups", "seq"), None),
        P(("groups", "seq"), None),
        P(("groups", "seq"), None),
        P(),
        P(),
        P(),
        P(),
    )
    out_specs = P(("groups", "seq"), None)
    return jax.shard_map(local, mesh=mesh, in_specs=in_specs, out_specs=out_specs, check_vma=False)
```
